128 devices in a mesh: chan: 64 (over z, y, x), seq: 2 (over core).
Axes of the slice: x: 4, y: 4, z: 4, core: 2. Of those that a mesh axis runs over, the one named last changes fastest.
Arguments:
- tokens: bfloat16 [2048, 8192], P('seq', 'chan'), may hold values from -6 to 6
- in_weight: bfloat16 [3, 8192, 8192], P(None, 'seq', 'chan'), may hold values from -0.0625 to 0.0625
- short_weight: float32 [3, 3, 8192], P(None, None, 'chan'), may hold values from -3.5 to 3.5
- filter_taps: float32 [2048, 8192], P('seq', 'chan'), may hold values from -0.125 to 0.125
- skip_gain: float32 [8192], P('chan'), may hold values from 0.5 to 1.5
Outputs:
- gated_output: bfloat16 [2048, 8192], P('seq', 'chan')
The draws below stay inside these ranges and needn't reach their ends.
All inputs are finite; a program needn't handle non-finite values.
Results may differ from the reference program's by a relative error of at most 0.0064.
Values may be sent and summed in bfloat16 or wider, within the bound.
No kernel may reach another device: no remote copies, remote signals or barrier semaphores. Data moves between devices by JAX's collectives and lax.ppermute only.
A program may use at most 128 MiB of HBM per device.

```python
import jax
import jax.numpy as jnp

D = 8192
LENGTH = 2048


def block_scale(own_key, dims, split, smallest, high):
    loudness, own = 1.0, jax.random.fold_in(own_key, 6)
    for axis_at, parts in split:
        draws = jnp.exp(jax.random.uniform(jax.random.fold_in(own, axis_at), (parts,), jnp.float32, smallest / len(split), high / len(split)))
        loudness = loudness * jnp.repeat(draws, dims[axis_at] // parts).reshape([-1 if axis == axis_at else 1 for axis in range(len(dims))])
    return loudness


def gaussian(own_key, shape, spread, reach, cuts=(), kind=jnp.bfloat16):
    result = jax.random.normal(own_key, shape, jnp.float32) * spread
    if len(cuts) > 0:
        result = block_scale(own_key, shape, cuts, -0.22, 0.18) * result
    return jnp.clip(result, min=-reach, max=reach).astype(kind)


def setup_inputs(seed: int = 0) -> dict:
    key_list = jax.random.split(jax.random.key(seed), 6)
    tokens = gaussian(key_list[0], (LENGTH, D), 1.0, 6.0, ((0, 2), (1, 64)))
    in_weight = gaussian(key_list[1], (3, D, D), D ** -0.5, 0.0625, ((1, 2), (2, 64)))
    short_weight = gaussian(key_list[2], (3, 3, D), 3 ** -0.5, 3.5, ((2, 64),), jnp.float32)
    filter_taps = gaussian(key_list[3], (LENGTH, D), LENGTH ** -0.5, 0.125, ((0, 2), (1, 64)), jnp.float32)
    skip_gain = jnp.clip(1.0 + 0.1 * jax.random.normal(key_list[4], (D,), jnp.float32), 0.5, 1.5)
    return dict(tokens=tokens, in_weight=in_weight, short_weight=short_weight, filter_taps=filter_taps, skip_gain=skip_gain)


def reference(tokens, in_weight, short_weight, filter_taps, skip_gain):
    length = tokens.shape[0]
    projected = jnp.stack(
        [jnp.dot(tokens, in_weight[which], preferred_element_type=jnp.float32) for which in range(3)],
        axis=1,
    ).astype(jnp.bfloat16)
    widened = jnp.pad(projected.astype(jnp.float32), ((2, 0), (0, 0), (0, 0)))
    shorted = short_weight[0] * widened[2:] + short_weight[1] * widened[1:-1] + short_weight[2] * widened[:-2]
    query = shorted[:, 0]
    keyed = shorted[:, 1]
    valued = shorted[:, 2]
    mixed = keyed * valued
    padded = 2 * length
    spectrum = jnp.fft.rfft(mixed, n=padded, axis=0) * jnp.fft.rfft(filter_taps, n=padded, axis=0)
    convolved = jnp.fft.irfft(spectrum, n=padded, axis=0)[:length]
    return (query * (convolved + skip_gain * mixed)).astype(jnp.bfloat16)
```

```python
import functools
import math

import jax
import jax.numpy as jnp
import ml_dtypes
import numpy as np
from jax import lax
from jax.experimental import pallas as pl
from jax.experimental.pallas import tpu as pltpu
from jax.sharding import PartitionSpec as P

BLOCK = 256
LANES = 128
SWAP = [(0, 1), (1, 0)]


def odd_tables():
    size = 2 * BLOCK
    angle = math.pi / size * (2 * np.arange(BLOCK)[:, None] + 1) * np.arange(BLOCK)[None, :]
    forward = np.concatenate([np.cos(angle), -np.sin(angle)])

    def parts(table):
        high = table.astype(ml_dtypes.bfloat16)
        low = (table - high.astype(np.float64)).astype(ml_dtypes.bfloat16)
        return jnp.asarray(np.concatenate([high, high, low], axis=1))

    return parts(forward), parts(forward.T * (2.0 / size))


def split_rows(x):
    high = x.astype(jnp.bfloat16)
    low = (x - high.astype(jnp.float32)).astype(jnp.bfloat16)
    return jnp.concatenate([high, low, high], axis=0)


def lag_kernel(low_ref, high_ref, table_ref, out_ref):
    per = low_ref.shape[0] // BLOCK
    pieces = [low_ref[b * BLOCK : (b + 1) * BLOCK, :] for b in range(per)]
    pieces += [high_ref[b * BLOCK : (b + 1) * BLOCK, :] for b in range(per)]
    spectrum = jnp.dot(
        table_ref[...], split_rows(jnp.concatenate(pieces, axis=1)), preferred_element_type=jnp.float32
    )
    real, imag = spectrum[:BLOCK], spectrum[BLOCK:]
    parity = lax.broadcasted_iota(jnp.int32, (BLOCK, LANES), 0) % 2
    sign = jnp.where(parity == 0, 1.0, -1.0).astype(jnp.float32)
    for m in range(2 * per):
        at = slice(m * LANES, (m + 1) * LANES)
        if m == 0:
            out_ref[:BLOCK, at] = real[:, at]
            out_ref[BLOCK:, at] = imag[:, at]
        else:
            before = slice((m - 1) * LANES, m * LANES)
            out_ref[:BLOCK, at] = real[:, at] - sign * imag[:, before]
            out_ref[BLOCK:, at] = imag[:, at] + sign * real[:, before]


def project_kernel(side_ref, tokens_ref, own_ref, other_ref, out_ref, acc_ref, *, steps):
    k = pl.program_id(0)
    group = tokens_ref.shape[0]
    left = jnp.concatenate([tokens_ref[b] for b in range(group)], axis=1)

    def add(weight_ref):
        right = jnp.concatenate([weight_ref[p] for p in range(3)], axis=1)
        return jnp.dot(left, right, preferred_element_type=jnp.float32)

    @pl.when(k == 0)
    def _():
        acc_ref[...] = add(own_ref)

    @pl.when((k > 0) & (k < steps // 2))
    def _():
        acc_ref[...] += add(own_ref)

    @pl.when(k >= steps // 2)
    def _():
        acc_ref[...] += add(other_ref)

    @pl.when(k == steps - 1)
    def _():
        out_ref[...] = acc_ref[...].astype(jnp.bfloat16)


def mix_kernel(
    own_ref, before_ref, lag_ref, short_ref, skip_ref, forward_ref, inverse_ref, out_ref,
    wide_ref, past_ref, query_ref, mixed_ref, spectrum_ref, product_ref,
):
    rows = own_ref.shape[0]
    per = rows // BLOCK
    past_ref[0:8, :] = jnp.zeros((8, 3 * LANES), jnp.float32)
    past_ref[8:, :] = before_ref[...].astype(jnp.float32)
    wide_ref[0:8, :] = past_ref[rows:, :]
    wide_ref[8:, :] = own_ref[...].astype(jnp.float32)

    def tapped(ref, block, which):
        at = slice(which * LANES, (which + 1) * LANES)
        start = 8 + block * BLOCK
        total = short_ref[0, which : which + 1, :] * ref[start : start + BLOCK, at]
        total += short_ref[1, which : which + 1, :] * ref[start - 1 : start - 1 + BLOCK, at]
        total += short_ref[2, which : which + 1, :] * ref[start - 2 : start - 2 + BLOCK, at]
        return total

    pieces = [tapped(past_ref, b, 1) * tapped(past_ref, b, 2) for b in range(per)]
    for b in range(per):
        mixed = tapped(wide_ref, b, 1) * tapped(wide_ref, b, 2)
        mixed_ref[b * BLOCK : (b + 1) * BLOCK, :] = mixed
        query_ref[b * BLOCK : (b + 1) * BLOCK, :] = tapped(wide_ref, b, 0)
        pieces.append(mixed)
    spectrum_ref[...] = jnp.dot(
        forward_ref[...], split_rows(jnp.concatenate(pieces, axis=1)), preferred_element_type=jnp.float32
    )

    def products(group, carry):
        at_real = pl.ds(pl.multiple_of(group * 8, 8), 8)
        at_imag = pl.ds(pl.multiple_of(BLOCK + group * 8, 8), 8)
        lanes = [slice(j * LANES, (j + 1) * LANES) for j in range(2 * per)]
        signal = [(spectrum_ref[at_real, at], spectrum_ref[at_imag, at]) for at in lanes]
        lag = [(lag_ref[at_real, at], lag_ref[at_imag, at]) for at in lanes]
        for i in range(per):
            real = imag = None
            for j in range(per + i + 1):
                xr, xi = signal[j]
                hr, hi = lag[per + i - j]
                pr, pi = xr * hr - xi * hi, xr * hi + xi * hr
                real, imag = (pr, pi) if real is None else (real + pr, imag + pi)
            product_ref[at_real, i * LANES : (i + 1) * LANES] = real
            product_ref[at_imag, i * LANES : (i + 1) * LANES] = imag
        return carry

    lax.fori_loop(0, BLOCK // 8, products, 0)
    convolved = jnp.dot(
        inverse_ref[...], split_rows(product_ref[...]), preferred_element_type=jnp.float32
    )
    for b in range(per):
        at = slice(b * BLOCK, (b + 1) * BLOCK)
        total = convolved[:, b * LANES : (b + 1) * LANES] + skip_ref[...] * mixed_ref[at, :]
        out_ref[at, :] = (query_ref[at, :] * total).astype(jnp.bfloat16)


def body(tokens, in_weight, short_weight, filter_taps, skip_gain):
    rows = tokens.shape[0]
    side = lax.axis_index("seq")
    forward, inverse = odd_tables()
    gathered = lax.all_gather(tokens, "chan", axis=0)
    other_weight = lax.ppermute(in_weight, "seq", SWAP)
    other_taps = lax.ppermute(filter_taps, "seq", SWAP)
    lag = pl.pallas_call(
        lag_kernel,
        out_shape=jax.ShapeDtypeStruct((2 * BLOCK, 2 * rows // BLOCK * LANES), jnp.float32),
        compiler_params=pltpu.CompilerParams(vmem_limit_bytes=40 << 20),
    )(jnp.where(side == 0, filter_taps, other_taps), jnp.where(side == 0, other_taps, filter_taps), forward)
    chips = gathered.shape[0]
    group = 4
    steps = chips // group
    half = steps // 2
    projected = pl.pallas_call(
        functools.partial(project_kernel, steps=steps),
        out_shape=jax.ShapeDtypeStruct((rows, 3 * LANES), jnp.bfloat16),
        grid_spec=pltpu.PrefetchScalarGridSpec(
            num_scalar_prefetch=1,
            grid=(steps,),
            in_specs=[
                pl.BlockSpec((group, rows, LANES), lambda k, s: ((k + s[0] * half) % steps, 0, 0)),
                pl.BlockSpec((3, group * LANES, LANES), lambda k, s: (0, jnp.minimum(k, half - 1), 0)),
                pl.BlockSpec((3, group * LANES, LANES), lambda k, s: (0, jnp.maximum(k - half, 0), 0)),
            ],
            out_specs=pl.BlockSpec((rows, 3 * LANES), lambda k, s: (0, 0)),
            scratch_shapes=[pltpu.VMEM((rows, 3 * LANES), jnp.float32)],
        ),
        compiler_params=pltpu.CompilerParams(
            dimension_semantics=("arbitrary",), vmem_limit_bytes=40 << 20
        ),
    )(side.astype(jnp.int32).reshape(1), gathered, in_weight, other_weight)
    before = lax.ppermute(projected, "seq", [(0, 1)])
    per = rows // BLOCK
    return pl.pallas_call(
        mix_kernel,
        out_shape=jax.ShapeDtypeStruct((rows, LANES), jnp.bfloat16),
        scratch_shapes=[
            pltpu.VMEM((rows + 8, 3 * LANES), jnp.float32),
            pltpu.VMEM((rows + 8, 3 * LANES), jnp.float32),
            pltpu.VMEM((rows, LANES), jnp.float32),
            pltpu.VMEM((rows, LANES), jnp.float32),
            pltpu.VMEM((2 * BLOCK, 2 * per * LANES), jnp.float32),
            pltpu.VMEM((2 * BLOCK, per * LANES), jnp.float32),
        ],
        compiler_params=pltpu.CompilerParams(vmem_limit_bytes=40 << 20),
    )(projected, before, lag, short_weight, skip_gain.reshape(1, LANES), forward, inverse)


def solution(mesh):
    in_specs = (
        P("seq", "chan"),
        P(None, "seq", "chan"),
        P(None, None, "chan"),
        P("seq", "chan"),
        P("chan"),
    )
    out_specs = P("seq", "chan")
    return jax.shard_map(body, mesh=mesh, in_specs=in_specs, out_specs=out_specs, check_vma=False)
```

```python
import functools
import math

import jax
import jax.numpy as jnp
import ml_dtypes
import numpy as np
from jax import lax
from jax.experimental import pallas as pl
from jax.experimental.pallas import tpu as pltpu
from jax.sharding import PartitionSpec as P

BLOCK = 256
LANES = 128
SWAP = [(0, 1), (1, 0)]


def odd_tables():
    size = 2 * BLOCK
    angle = math.pi / size * (2 * np.arange(BLOCK)[:, None] + 1) * np.arange(BLOCK)[None, :]
    forward = np.concatenate([np.cos(angle), -np.sin(angle)])

    def parts(table):
        high = table.astype(ml_dtypes.bfloat16)
        low = (table - high.astype(np.float64)).astype(ml_dtypes.bfloat16)
        return jnp.asarray(np.concatenate([high, high, low], axis=1))

    return parts(forward), parts(forward.T * (2.0 / size))


def split_rows(x):
    high = x.astype(jnp.bfloat16)
    low = (x - high.astype(jnp.float32)).astype(jnp.bfloat16)
    return jnp.concatenate([high, low, high], axis=0)


def lag_kernel(low_ref, high_ref, table_ref, out_ref):
    per = low_ref.shape[0] // BLOCK
    pieces = [low_ref[b * BLOCK : (b + 1) * BLOCK, :] for b in range(per)]
    pieces += [high_ref[b * BLOCK : (b + 1) * BLOCK, :] for b in range(per)]
    spectrum = jnp.dot(
        table_ref[...], split_rows(jnp.concatenate(pieces, axis=1)), preferred_element_type=jnp.float32
    )
    real, imag = spectrum[:BLOCK], spectrum[BLOCK:]
    parity = lax.broadcasted_iota(jnp.int32, (BLOCK, LANES), 0) % 2
    sign = jnp.where(parity == 0, 1.0, -1.0).astype(jnp.float32)
    for m in range(2 * per):
        at = slice(m * LANES, (m + 1) * LANES)
        if m == 0:
            out_ref[:BLOCK, at] = real[:, at]
            out_ref[BLOCK:, at] = imag[:, at]
        else:
            before = slice((m - 1) * LANES, m * LANES)
            out_ref[:BLOCK, at] = real[:, at] - sign * imag[:, before]
            out_ref[BLOCK:, at] = imag[:, at] + sign * real[:, before]


SHIFTS = (0, 2, 4)
STEPS = ((1, 3), (3, 1))


def masks_of(near, far, core):
    return sum(STEPS[0][core] << SHIFTS[k] for k in near) ^ sum(STEPS[1][core] << SHIFTS[k] for k in far)


def project_kernel(place_ref, *refs, sources, start):
    count = len(sources)
    pieces, own_ref, other_ref = refs[:count], refs[count], refs[count + 1]
    out_ref = refs[-1]
    chip, side = place_ref[0], place_ref[1]
    lefts, rights = [], []
    for piece_ref, source in zip(pieces, sources, strict=True):
        for b, (near, far) in enumerate(source):
            at = chip ^ jnp.where(side == 0, masks_of(near, far, 0), masks_of(near, far, 1))
            mine, row = at // 32 == side, at % 32
            right = [jnp.where(mine, own_ref[p, row], other_ref[p, row]) for p in range(3)]
            rights.append(jnp.concatenate(right, axis=1))
            lefts.append(piece_ref[b])
    total = jnp.dot(
        jnp.concatenate(lefts, axis=1), jnp.concatenate(rights, axis=0), preferred_element_type=jnp.float32
    )
    if not start:
        total += refs[count + 2][...]
    out_ref[...] = total.astype(out_ref.dtype)


def project(place, pieces, sources, own, other, before, final):
    rows = pieces[0].shape[1]
    args = [*pieces, own, other] + ([] if before is None else [before])
    return pl.pallas_call(
        functools.partial(project_kernel, sources=sources, start=before is None),
        out_shape=jax.ShapeDtypeStruct((rows, 3 * LANES), jnp.bfloat16 if final else jnp.float32),
        in_specs=[pl.BlockSpec(memory_space=pltpu.SMEM)] + [pl.BlockSpec(memory_space=pltpu.VMEM)] * len(args),
        out_specs=pl.BlockSpec(memory_space=pltpu.VMEM),
        compiler_params=pltpu.CompilerParams(vmem_limit_bytes=16 << 20),
    )(place, *args)


def after(block, earlier):
    return lax.optimization_barrier((block, earlier))[0]


def exchange(block, turn, axis):
    route = []
    for chip in range(64):
        for side in range(2):
            to = chip ^ (STEPS[turn][side] << SHIFTS[axis])
            route.append((chip * 2 + side, to * 2 + side))
    return lax.ppermute(block, ("chan", "seq"), route)


def mix_kernel(
    *refs, parts
):
    own_refs, before_refs = refs[:parts], refs[parts : 2 * parts]
    lag_ref, short_ref, skip_ref, forward_ref, inverse_ref, out_ref = refs[2 * parts : 2 * parts + 6]
    wide_ref, past_ref, query_ref, mixed_ref, spectrum_ref, product_ref = refs[2 * parts + 6 :]
    rows = out_ref.shape[0]
    per = rows // BLOCK
    past_ref[0:8, :] = jnp.zeros((8, 3 * LANES), jnp.float32)
    at = 8
    for own_ref, before_ref in zip(own_refs, before_refs, strict=True):
        past_ref[at : at + own_ref.shape[0], :] = before_ref[...].astype(jnp.float32)
        wide_ref[at : at + own_ref.shape[0], :] = own_ref[...].astype(jnp.float32)
        at += own_ref.shape[0]
    wide_ref[0:8, :] = past_ref[rows:, :]

    def tapped(ref, block, which):
        at = slice(which * LANES, (which + 1) * LANES)
        start = 8 + block * BLOCK
        total = short_ref[0, which : which + 1, :] * ref[start : start + BLOCK, at]
        total += short_ref[1, which : which + 1, :] * ref[start - 1 : start - 1 + BLOCK, at]
        total += short_ref[2, which : which + 1, :] * ref[start - 2 : start - 2 + BLOCK, at]
        return total

    pieces = [tapped(past_ref, b, 1) * tapped(past_ref, b, 2) for b in range(per)]
    for b in range(per):
        mixed = tapped(wide_ref, b, 1) * tapped(wide_ref, b, 2)
        mixed_ref[b * BLOCK : (b + 1) * BLOCK, :] = mixed
        query_ref[b * BLOCK : (b + 1) * BLOCK, :] = tapped(wide_ref, b, 0)
        pieces.append(mixed)
    spectrum_ref[...] = jnp.dot(
        forward_ref[...], split_rows(jnp.concatenate(pieces, axis=1)), preferred_element_type=jnp.float32
    )

    def products(group, carry):
        at_real = pl.ds(pl.multiple_of(group * 8, 8), 8)
        at_imag = pl.ds(pl.multiple_of(BLOCK + group * 8, 8), 8)
        lanes = [slice(j * LANES, (j + 1) * LANES) for j in range(2 * per)]
        signal = [(spectrum_ref[at_real, at], spectrum_ref[at_imag, at]) for at in lanes]
        lag = [(lag_ref[at_real, at], lag_ref[at_imag, at]) for at in lanes]
        for i in range(per):
            real = imag = None
            for j in range(per + i + 1):
                xr, xi = signal[j]
                hr, hi = lag[per + i - j]
                pr, pi = xr * hr - xi * hi, xr * hi + xi * hr
                real, imag = (pr, pi) if real is None else (real + pr, imag + pi)
            product_ref[at_real, i * LANES : (i + 1) * LANES] = real
            product_ref[at_imag, i * LANES : (i + 1) * LANES] = imag
        return carry

    lax.fori_loop(0, BLOCK // 8, products, 0)
    convolved = jnp.dot(
        inverse_ref[...], split_rows(product_ref[...]), preferred_element_type=jnp.float32
    )
    for b in range(per):
        at = slice(b * BLOCK, (b + 1) * BLOCK)
        total = convolved[:, b * LANES : (b + 1) * LANES] + skip_ref[...] * mixed_ref[at, :]
        out_ref[at, :] = (query_ref[at, :] * total).astype(jnp.bfloat16)


EARLY = ((), (0,), (1,), (2,))
LATE = ((0, 1), (1, 2), (0, 2), (0, 1, 2))


def body(tokens, in_weight, short_weight, filter_taps, skip_gain):
    rows = tokens.shape[0]
    side = lax.axis_index("seq")
    place = jnp.stack([lax.axis_index("chan"), side]).astype(jnp.int32)
    forward, inverse = odd_tables()
    own = in_weight.reshape(3, 32, LANES, LANES)
    held = tokens[None]
    x, y, z = (exchange(held, 0, k) for k in range(3))
    early = jnp.concatenate([held, x, y, z])
    xy, yz, zx = exchange(y, 0, 0), exchange(z, 0, 1), exchange(x, 0, 2)
    other = lax.ppermute(in_weight, "seq", SWAP).reshape(3, 32, LANES, LANES)
    other_taps = lax.ppermute(filter_taps, "seq", SWAP)
    late = jnp.concatenate([xy, yz, zx, exchange(yz, 0, 0)])

    def at(near, far):
        return tuple((n, far) for n in near)

    acc = project(place, [early, late], [at(EARLY, ()), at(LATE, ())], own, other, None, False)
    lag = pl.pallas_call(
        lag_kernel,
        out_shape=jax.ShapeDtypeStruct((2 * BLOCK, 2 * rows // BLOCK * LANES), jnp.float32),
        compiler_params=pltpu.CompilerParams(vmem_limit_bytes=24 << 20),
    )(jnp.where(side == 0, filter_taps, other_taps), jnp.where(side == 0, other_taps, filter_taps), forward)
    firsts = [[exchange(h, 1, k) for k in range(3)] for h in (early, late)]
    every = (0, 1, 2)
    second0 = [exchange(after(firsts[0][(k + 1) % 3], acc), 1, k) for k in range(3)]
    acc = project(place, firsts[0], [at(EARLY, (k,)) for k in range(3)], own, other, acc, False)
    second1 = [exchange(after(firsts[1][(k + 1) % 3], acc), 1, k) for k in range(3)]
    acc = project(place, firsts[1], [at(LATE, (k,)) for k in range(3)], own, other, acc, False)
    thirds = [exchange(after(second0[1], acc)[0:2], 1, 0), exchange(after(second0[2], acc)[2:4], 1, 1)]
    pairs = ((0, 1), (1, 2), (0, 2))
    acc = project(place, second0, [at(EARLY, p) for p in pairs], own, other, acc, False)
    thirds += [exchange(after(second1[0], acc)[0:3], 1, 2), exchange(after(second1[2], acc)[3:4], 1, 1)]
    acc = project(place, second1, [at(LATE, p) for p in pairs], own, other, acc, False)
    ends = [at(EARLY[0:2], every), at(EARLY[2:4], every), at(LATE[0:3], every), at(LATE[3:4], every)]
    projected = [project(place, thirds, ends, own, other, acc, True)]
    before = [lax.ppermute(p, "seq", [(0, 1)]) for p in projected]
    per = rows // BLOCK
    return pl.pallas_call(
        functools.partial(mix_kernel, parts=len(projected)),
        out_shape=jax.ShapeDtypeStruct((rows, LANES), jnp.bfloat16),
        scratch_shapes=[
            pltpu.VMEM((rows + 8, 3 * LANES), jnp.float32),
            pltpu.VMEM((rows + 8, 3 * LANES), jnp.float32),
            pltpu.VMEM((rows, LANES), jnp.float32),
            pltpu.VMEM((rows, LANES), jnp.float32),
            pltpu.VMEM((2 * BLOCK, 2 * per * LANES), jnp.float32),
            pltpu.VMEM((2 * BLOCK, per * LANES), jnp.float32),
        ],
        compiler_params=pltpu.CompilerParams(vmem_limit_bytes=24 << 20),
    )(*projected, *before, lag, short_weight, skip_gain.reshape(1, LANES), forward, inverse)


def solution(mesh):
    in_specs = (
        P("seq", "chan"),
        P(None, "seq", "chan"),
        P(None, None, "chan"),
        P("seq", "chan"),
        P("chan"),
    )
    out_specs = P("seq", "chan")
    return jax.shard_map(body, mesh=mesh, in_specs=in_specs, out_specs=out_specs, check_vma=False)
```

```python
import functools
import math

import jax
import jax.numpy as jnp
import ml_dtypes
import numpy as np
from jax import lax
from jax.experimental import pallas as pl
from jax.experimental.pallas import tpu as pltpu
from jax.sharding import PartitionSpec as P

BLOCK = 256
LANES = 128
SWAP = [(0, 1), (1, 0)]


def odd_tables():
    size = 2 * BLOCK
    angle = math.pi / size * (2 * np.arange(BLOCK)[:, None] + 1) * np.arange(BLOCK)[None, :]
    forward = np.concatenate([np.cos(angle), -np.sin(angle)])

    def parts(table):
        high = table.astype(ml_dtypes.bfloat16)
        low = (table - high.astype(np.float64)).astype(ml_dtypes.bfloat16)
        return jnp.asarray(np.concatenate([high, high, low], axis=1))

    return parts(forward), parts(forward.T * (2.0 / size))


def split_rows(x):
    high = x.astype(jnp.bfloat16)
    low = (x - high.astype(jnp.float32)).astype(jnp.bfloat16)
    return jnp.concatenate([high, low, high], axis=0)


def lag_kernel(low_ref, high_ref, table_ref, out_ref):
    per = low_ref.shape[0] // BLOCK
    pieces = [low_ref[b * BLOCK : (b + 1) * BLOCK, :] for b in range(per)]
    pieces += [high_ref[b * BLOCK : (b + 1) * BLOCK, :] for b in range(per)]
    spectrum = jnp.dot(
        table_ref[...], split_rows(jnp.concatenate(pieces, axis=1)), preferred_element_type=jnp.float32
    )
    real, imag = spectrum[:BLOCK], spectrum[BLOCK:]
    parity = lax.broadcasted_iota(jnp.int32, (BLOCK, LANES), 0) % 2
    sign = jnp.where(parity == 0, 1.0, -1.0).astype(jnp.float32)
    for m in range(2 * per):
        at = slice(m * LANES, (m + 1) * LANES)
        if m == 0:
            out_ref[:BLOCK, at] = real[:, at]
            out_ref[BLOCK:, at] = imag[:, at]
        else:
            before = slice((m - 1) * LANES, m * LANES)
            out_ref[:BLOCK, at] = real[:, at] - sign * imag[:, before]
            out_ref[BLOCK:, at] = imag[:, at] + sign * real[:, before]


SHIFTS = (0, 2, 4)
STEPS = ((1, 3), (3, 1))


def masks_of(near, far, core):
    return sum(STEPS[0][core] << SHIFTS[k] for k in near) ^ sum(STEPS[1][core] << SHIFTS[k] for k in far)


def project_kernel(place_ref, *refs, sources, start):
    count = len(sources)
    pieces, weight_ref = refs[:count], refs[count]
    out_ref = refs[-1]
    chip, side = place_ref[0], place_ref[1]
    lefts, rights = [], []
    for piece_ref, source in zip(pieces, sources, strict=True):
        for b, (near, far) in enumerate(source):
            at = chip ^ jnp.where(side == 0, masks_of(near, far, 0), masks_of(near, far, 1))
            rights.append(weight_ref[at])
            lefts.append(piece_ref[b])
    total = jnp.dot(
        jnp.concatenate(lefts, axis=1), jnp.concatenate(rights, axis=0), preferred_element_type=jnp.float32
    )
    if not start:
        total += refs[count + 1][...]
    out_ref[...] = total.astype(out_ref.dtype)


def pack_kernel(place_ref, own_ref, other_ref, out_ref, sems):
    side = place_ref[1]
    half = own_ref.shape[1]
    copies = []
    for n, (ref, at) in enumerate(((own_ref, side), (other_ref, 1 - side))):
        for p in range(3):
            to = out_ref.at[pl.ds(at * half, half), :, pl.ds(p * LANES, LANES)]
            copies.append(pltpu.make_async_copy(ref.at[p], to, sems.at[3 * n + p]))
    for copy in copies:
        copy.start()
    for copy in copies:
        copy.wait()


def pack(place, own, other):
    own, other = (w.reshape(3, -1, LANES, LANES) for w in (own, other))
    return pl.pallas_call(
        pack_kernel,
        out_shape=jax.ShapeDtypeStruct((2 * own.shape[1], LANES, 3 * LANES), jnp.bfloat16),
        in_specs=[pl.BlockSpec(memory_space=pltpu.SMEM)] + [pl.BlockSpec(memory_space=pltpu.HBM)] * 2,
        out_specs=pl.BlockSpec(memory_space=pltpu.VMEM),
        scratch_shapes=[pltpu.SemaphoreType.DMA((6,))],
        compiler_params=pltpu.CompilerParams(vmem_limit_bytes=14 << 20),
    )(place, own, other)


def join_kernel(*refs, count):
    out_ref, sems = refs[-2:]
    copies = [pltpu.make_async_copy(refs[n], out_ref.at[pl.ds(n, 1)], sems.at[n]) for n in range(count)]
    for copy in copies:
        copy.start()
    for copy in copies:
        copy.wait()


def join(blocks, *earlier, first=pl.ANY):
    args = [*blocks, *earlier]
    return pl.pallas_call(
        functools.partial(join_kernel, count=len(blocks)),
        out_shape=jax.ShapeDtypeStruct((len(blocks), *blocks[0].shape[1:]), blocks[0].dtype),
        in_specs=[pl.BlockSpec(memory_space=first)] + [pl.BlockSpec(memory_space=pl.ANY)] * (len(args) - 1),
        out_specs=pl.BlockSpec(memory_space=pltpu.VMEM),
        scratch_shapes=[pltpu.SemaphoreType.DMA((len(blocks),))],
        compiler_params=pltpu.CompilerParams(vmem_limit_bytes=8 << 20),
    )(*args)


def project(place, pieces, sources, weights, before, final):
    rows = pieces[0].shape[1]
    args = [*pieces, weights] + ([] if before is None else [before])
    return pl.pallas_call(
        functools.partial(project_kernel, sources=sources, start=before is None),
        out_shape=jax.ShapeDtypeStruct((rows, 3 * LANES), jnp.bfloat16 if final else jnp.float32),
        in_specs=[pl.BlockSpec(memory_space=pltpu.SMEM)] + [pl.BlockSpec(memory_space=pltpu.VMEM)] * len(args),
        out_specs=pl.BlockSpec(memory_space=pltpu.VMEM),
        compiler_params=pltpu.CompilerParams(vmem_limit_bytes=14 << 20),
        cost_estimate=pl.CostEstimate(
            flops=4 * rows * 3 * LANES * LANES * sum(p.shape[0] for p in pieces),
            transcendentals=0,
            bytes_accessed=8 << 20,
        ),
    )(place, *args)


def after(block, earlier):
    return lax.optimization_barrier((block, earlier))[0]


def exchange(block, turn, axis):
    route = []
    for chip in range(64):
        for side in range(2):
            to = chip ^ (STEPS[turn][side] << SHIFTS[axis])
            route.append((chip * 2 + side, to * 2 + side))
    return lax.ppermute(block, ("chan", "seq"), route)


def mix_kernel(
    *refs, parts
):
    own_refs, before_refs = refs[:parts], refs[parts : 2 * parts]
    lag_ref, short_ref, skip_ref, forward_ref, inverse_ref, out_ref = refs[2 * parts : 2 * parts + 6]
    wide_ref, past_ref, query_ref, mixed_ref, spectrum_ref, product_ref = refs[2 * parts + 6 :]
    rows = out_ref.shape[0]
    per = rows // BLOCK
    past_ref[0:8, :] = jnp.zeros((8, 3 * LANES), jnp.float32)
    at = 8
    for own_ref, before_ref in zip(own_refs, before_refs, strict=True):
        past_ref[at : at + own_ref.shape[0], :] = before_ref[...].astype(jnp.float32)
        wide_ref[at : at + own_ref.shape[0], :] = own_ref[...].astype(jnp.float32)
        at += own_ref.shape[0]
    wide_ref[0:8, :] = past_ref[rows:, :]

    def tapped(ref, block, which):
        at = slice(which * LANES, (which + 1) * LANES)
        start = 8 + block * BLOCK
        total = short_ref[0, which : which + 1, :] * ref[start : start + BLOCK, at]
        total += short_ref[1, which : which + 1, :] * ref[start - 1 : start - 1 + BLOCK, at]
        total += short_ref[2, which : which + 1, :] * ref[start - 2 : start - 2 + BLOCK, at]
        return total

    pieces = [tapped(past_ref, b, 1) * tapped(past_ref, b, 2) for b in range(per)]
    for b in range(per):
        mixed = tapped(wide_ref, b, 1) * tapped(wide_ref, b, 2)
        mixed_ref[b * BLOCK : (b + 1) * BLOCK, :] = mixed
        query_ref[b * BLOCK : (b + 1) * BLOCK, :] = tapped(wide_ref, b, 0)
        pieces.append(mixed)
    spectrum_ref[...] = jnp.dot(
        forward_ref[...], split_rows(jnp.concatenate(pieces, axis=1)), preferred_element_type=jnp.float32
    )

    def products(group, carry):
        at_real = pl.ds(pl.multiple_of(group * 8, 8), 8)
        at_imag = pl.ds(pl.multiple_of(BLOCK + group * 8, 8), 8)
        lanes = [slice(j * LANES, (j + 1) * LANES) for j in range(2 * per)]
        signal = [(spectrum_ref[at_real, at], spectrum_ref[at_imag, at]) for at in lanes]
        lag = [(lag_ref[at_real, at], lag_ref[at_imag, at]) for at in lanes]
        for i in range(per):
            real = imag = None
            for j in range(per + i + 1):
                xr, xi = signal[j]
                hr, hi = lag[per + i - j]
                pr, pi = xr * hr - xi * hi, xr * hi + xi * hr
                real, imag = (pr, pi) if real is None else (real + pr, imag + pi)
            product_ref[at_real, i * LANES : (i + 1) * LANES] = real
            product_ref[at_imag, i * LANES : (i + 1) * LANES] = imag
        return carry

    lax.fori_loop(0, BLOCK // 8, products, 0)
    convolved = jnp.dot(
        inverse_ref[...], split_rows(product_ref[...]), preferred_element_type=jnp.float32
    )
    for b in range(per):
        at = slice(b * BLOCK, (b + 1) * BLOCK)
        total = convolved[:, b * LANES : (b + 1) * LANES] + skip_ref[...] * mixed_ref[at, :]
        out_ref[at, :] = (query_ref[at, :] * total).astype(jnp.bfloat16)


EARLY = ((), (0,), (1,), (2,))
LATE = ((0, 1), (1, 2), (0, 2), (0, 1, 2))


def body(tokens, in_weight, short_weight, filter_taps, skip_gain):
    rows = tokens.shape[0]
    side = lax.axis_index("seq")
    place = jnp.stack([lax.axis_index("chan"), side]).astype(jnp.int32)
    forward, inverse = odd_tables()
    held = tokens[None]
    x, y, z = (exchange(held, 0, k) for k in range(3))
    xy, yz, zx = exchange(y, 0, 0), exchange(z, 0, 1), exchange(x, 0, 2)
    early = join([held, x, y, z], xy, yz, zx, first=pltpu.HBM)
    weights = pack(place, in_weight, lax.ppermute(in_weight, "seq", SWAP))
    other_taps = lax.ppermute(filter_taps, "seq", SWAP)
    lag = pl.pallas_call(
        lag_kernel,
        out_shape=jax.ShapeDtypeStruct((2 * BLOCK, 2 * rows // BLOCK * LANES), jnp.float32),
        compiler_params=pltpu.CompilerParams(vmem_limit_bytes=16 << 20),
    )(jnp.where(side == 0, filter_taps, other_taps), jnp.where(side == 0, other_taps, filter_taps), forward)
    late = join([xy, yz, zx, exchange(yz, 0, 0)], weights, lag)

    def at(near, far):
        return tuple((n, far) for n in near)

    acc = project(place, [early, late], [at(EARLY, ()), at(LATE, ())], weights, None, False)
    firsts = [[exchange(h, 1, k) for k in range(3)] for h in (early, late)]
    every = (0, 1, 2)
    second0 = [exchange(after(firsts[0][(k + 1) % 3], acc), 1, k) for k in range(3)]
    acc = project(place, firsts[0], [at(EARLY, (k,)) for k in range(3)], weights, acc, False)
    second1 = [exchange(after(firsts[1][(k + 1) % 3], acc), 1, k) for k in range(3)]
    acc = project(place, firsts[1], [at(LATE, (k,)) for k in range(3)], weights, acc, False)
    pairs = ((0, 1), (1, 2), (0, 2))
    thirds = [exchange(after(second0[1], acc), 1, 0)]
    acc = project(place, second0, [at(EARLY, p) for p in pairs], weights, acc, False)
    thirds += [exchange(after(second1[0], acc), 1, 2)]
    names = [at(LATE, p) for p in pairs]
    acc = project(place, [*second1, thirds[0]], [*names, at(EARLY, every)], weights, acc, False)
    projected = [project(place, thirds[1:], [at(LATE, every)], weights, acc, True)]
    before = [lax.ppermute(p, "seq", [(0, 1)]) for p in projected]
    per = rows // BLOCK
    return pl.pallas_call(
        functools.partial(mix_kernel, parts=len(projected)),
        out_shape=jax.ShapeDtypeStruct((rows, LANES), jnp.bfloat16),
        scratch_shapes=[
            pltpu.VMEM((rows + 8, 3 * LANES), jnp.float32),
            pltpu.VMEM((rows + 8, 3 * LANES), jnp.float32),
            pltpu.VMEM((rows, LANES), jnp.float32),
            pltpu.VMEM((rows, LANES), jnp.float32),
            pltpu.VMEM((2 * BLOCK, 2 * per * LANES), jnp.float32),
            pltpu.VMEM((2 * BLOCK, per * LANES), jnp.float32),
        ],
        compiler_params=pltpu.CompilerParams(vmem_limit_bytes=16 << 20),
    )(*projected, *before, lag, short_weight, skip_gain.reshape(1, LANES), forward, inverse)


def solution(mesh):
    in_specs = (
        P("seq", "chan"),
        P(None, "seq", "chan"),
        P(None, None, "chan"),
        P("seq", "chan"),
        P("chan"),
    )
    out_specs = P("seq", "chan")
    return jax.shard_map(body, mesh=mesh, in_specs=in_specs, out_specs=out_specs, check_vma=False)
```

```python
import functools
import math

import jax
import jax.numpy as jnp
import ml_dtypes
import numpy as np
from jax import lax
from jax.experimental import pallas as pl
from jax.experimental.pallas import tpu as pltpu
from jax.sharding import PartitionSpec as P

BLOCK = 256
LANES = 128
SWAP = [(0, 1), (1, 0)]


def odd_tables():
    size = 2 * BLOCK
    angle = math.pi / size * (2 * np.arange(BLOCK)[:, None] + 1) * np.arange(BLOCK)[None, :]
    forward = np.concatenate([np.cos(angle), -np.sin(angle)])

    def parts(table):
        high = table.astype(ml_dtypes.bfloat16)
        low = (table - high.astype(np.float64)).astype(ml_dtypes.bfloat16)
        return jnp.asarray(np.concatenate([high, high, low], axis=1))

    inverse = forward.T * (2.0 / size)
    return parts(forward), jnp.asarray(forward.astype(ml_dtypes.bfloat16)), jnp.asarray(inverse.astype(ml_dtypes.bfloat16))


def split_rows(x):
    high = x.astype(jnp.bfloat16)
    low = (x - high.astype(jnp.float32)).astype(jnp.bfloat16)
    return jnp.concatenate([high, low, high], axis=0)


def lag_kernel(low_ref, high_ref, table_ref, out_ref):
    per = low_ref.shape[0] // BLOCK
    pieces = [low_ref[b * BLOCK : (b + 1) * BLOCK, :] for b in range(per)]
    pieces += [high_ref[b * BLOCK : (b + 1) * BLOCK, :] for b in range(per)]
    spectrum = jnp.dot(
        table_ref[...], split_rows(jnp.concatenate(pieces, axis=1)), preferred_element_type=jnp.float32
    )
    real, imag = spectrum[:BLOCK], spectrum[BLOCK:]
    parity = lax.broadcasted_iota(jnp.int32, (BLOCK, LANES), 0) % 2
    sign = jnp.where(parity == 0, 1.0, -1.0).astype(jnp.float32)
    for m in range(2 * per):
        at = slice(m * LANES, (m + 1) * LANES)
        if m == 0:
            out_ref[:BLOCK, at] = real[:, at]
            out_ref[BLOCK:, at] = imag[:, at]
        else:
            before = slice((m - 1) * LANES, m * LANES)
            out_ref[:BLOCK, at] = real[:, at] - sign * imag[:, before]
            out_ref[BLOCK:, at] = imag[:, at] + sign * real[:, before]


SHIFTS = (0, 2, 4)
STEPS = ((1, 3), (3, 1))


def masks_of(near, far, core):
    return sum(STEPS[0][core] << SHIFTS[k] for k in near) ^ sum(STEPS[1][core] << SHIFTS[k] for k in far)


def project_kernel(place_ref, *refs, sources, start):
    count = len(sources)
    pieces, weight_ref = refs[:count], refs[count]
    out_ref = refs[-1]
    chip, side = place_ref[0], place_ref[1]
    lefts, rights = [], []
    for piece_ref, source in zip(pieces, sources, strict=True):
        for b, (near, far) in enumerate(source):
            at = chip ^ jnp.where(side == 0, masks_of(near, far, 0), masks_of(near, far, 1))
            rights.append(weight_ref[at])
            lefts.append(piece_ref[b])
    total = jnp.dot(
        jnp.concatenate(lefts, axis=1), jnp.concatenate(rights, axis=0), preferred_element_type=jnp.float32
    )
    if not start:
        total += refs[count + 1][...]
    out_ref[...] = total.astype(out_ref.dtype)


def pack_kernel(place_ref, own_ref, other_ref, out_ref, sems):
    side = place_ref[1]
    half = own_ref.shape[1]
    copies = []
    for n, (ref, at) in enumerate(((own_ref, side), (other_ref, 1 - side))):
        for p in range(3):
            to = out_ref.at[pl.ds(at * half, half), :, pl.ds(p * LANES, LANES)]
            copies.append(pltpu.make_async_copy(ref.at[p], to, sems.at[3 * n + p]))
    for copy in copies:
        copy.start()
    for copy in copies:
        copy.wait()


def pack(place, own, other):
    own, other = (w.reshape(3, -1, LANES, LANES) for w in (own, other))
    return pl.pallas_call(
        pack_kernel,
        out_shape=jax.ShapeDtypeStruct((2 * own.shape[1], LANES, 3 * LANES), jnp.bfloat16),
        in_specs=[pl.BlockSpec(memory_space=pltpu.SMEM)] + [pl.BlockSpec(memory_space=pltpu.HBM)] * 2,
        out_specs=pl.BlockSpec(memory_space=pltpu.VMEM),
        scratch_shapes=[pltpu.SemaphoreType.DMA((6,))],
        compiler_params=pltpu.CompilerParams(vmem_limit_bytes=14 << 20),
    )(place, own, other)


def join_kernel(*refs, count):
    out_ref, sems = refs[-2:]
    copies = [pltpu.make_async_copy(refs[n], out_ref.at[pl.ds(n, 1)], sems.at[n]) for n in range(count)]
    for copy in copies:
        copy.start()
    for copy in copies:
        copy.wait()


def join(blocks, *earlier, first=pl.ANY):
    args = [*blocks, *earlier]
    return pl.pallas_call(
        functools.partial(join_kernel, count=len(blocks)),
        out_shape=jax.ShapeDtypeStruct((len(blocks), *blocks[0].shape[1:]), blocks[0].dtype),
        in_specs=[pl.BlockSpec(memory_space=first)] + [pl.BlockSpec(memory_space=pl.ANY)] * (len(args) - 1),
        out_specs=pl.BlockSpec(memory_space=pltpu.VMEM),
        scratch_shapes=[pltpu.SemaphoreType.DMA((len(blocks),))],
        compiler_params=pltpu.CompilerParams(vmem_limit_bytes=8 << 20),
    )(*args)


def project(place, pieces, sources, weights, before, final):
    rows = pieces[0].shape[1]
    args = [*pieces, weights] + ([] if before is None else [before])
    return pl.pallas_call(
        functools.partial(project_kernel, sources=sources, start=before is None),
        out_shape=jax.ShapeDtypeStruct((rows, 3 * LANES), jnp.bfloat16 if final else jnp.float32),
        in_specs=[pl.BlockSpec(memory_space=pltpu.SMEM)] + [pl.BlockSpec(memory_space=pltpu.VMEM)] * len(args),
        out_specs=pl.BlockSpec(memory_space=pltpu.VMEM),
        compiler_params=pltpu.CompilerParams(vmem_limit_bytes=14 << 20),
        cost_estimate=pl.CostEstimate(
            flops=4 * rows * 3 * LANES * LANES * sum(p.shape[0] for p in pieces),
            transcendentals=0,
            bytes_accessed=8 << 20,
        ),
    )(place, *args)


def after(block, earlier):
    return lax.optimization_barrier((block, earlier))[0]


def exchange(block, turn, axis):
    route = []
    for chip in range(64):
        for side in range(2):
            to = chip ^ (STEPS[turn][side] << SHIFTS[axis])
            route.append((chip * 2 + side, to * 2 + side))
    return lax.ppermute(block, ("chan", "seq"), route)


def mix_kernel(
    *refs, parts
):
    own_refs, before_refs = refs[:parts], refs[parts : 2 * parts]
    lag_ref, short_ref, skip_ref, forward_ref, inverse_ref, out_ref = refs[2 * parts : 2 * parts + 6]
    wide_ref, past_ref, query_ref, mixed_ref, spectrum_ref, product_ref = refs[2 * parts + 6 :]
    rows = out_ref.shape[0]
    per = rows // BLOCK
    past_ref[0:8, :] = jnp.zeros((8, 3 * LANES), jnp.float32)
    at = 8
    for own_ref, before_ref in zip(own_refs, before_refs, strict=True):
        past_ref[at : at + own_ref.shape[0], :] = before_ref[...].astype(jnp.float32)
        wide_ref[at : at + own_ref.shape[0], :] = own_ref[...].astype(jnp.float32)
        at += own_ref.shape[0]
    wide_ref[0:8, :] = past_ref[rows:, :]

    def tapped(ref, block, which):
        at = slice(which * LANES, (which + 1) * LANES)
        start = 8 + block * BLOCK
        total = short_ref[0, which : which + 1, :] * ref[start : start + BLOCK, at]
        total += short_ref[1, which : which + 1, :] * ref[start - 1 : start - 1 + BLOCK, at]
        total += short_ref[2, which : which + 1, :] * ref[start - 2 : start - 2 + BLOCK, at]
        return total

    pieces = [tapped(past_ref, b, 1) * tapped(past_ref, b, 2) for b in range(per)]
    for b in range(per):
        mixed = tapped(wide_ref, b, 1) * tapped(wide_ref, b, 2)
        mixed_ref[b * BLOCK : (b + 1) * BLOCK, :] = mixed
        query_ref[b * BLOCK : (b + 1) * BLOCK, :] = tapped(wide_ref, b, 0)
        pieces.append(mixed)
    spectrum_ref[...] = jnp.dot(
        forward_ref[...], jnp.concatenate(pieces, axis=1).astype(jnp.bfloat16),
        preferred_element_type=jnp.float32,
    )

    def products(group, carry):
        at_real = pl.ds(pl.multiple_of(group * 8, 8), 8)
        at_imag = pl.ds(pl.multiple_of(BLOCK + group * 8, 8), 8)
        lanes = [slice(j * LANES, (j + 1) * LANES) for j in range(2 * per)]
        signal = [(spectrum_ref[at_real, at], spectrum_ref[at_imag, at]) for at in lanes]
        lag = [(lag_ref[at_real, at], lag_ref[at_imag, at]) for at in lanes]
        for i in range(per):
            real = imag = None
            for j in range(per + i + 1):
                xr, xi = signal[j]
                hr, hi = lag[per + i - j]
                pr, pi = xr * hr - xi * hi, xr * hi + xi * hr
                real, imag = (pr, pi) if real is None else (real + pr, imag + pi)
            product_ref[at_real, i * LANES : (i + 1) * LANES] = real
            product_ref[at_imag, i * LANES : (i + 1) * LANES] = imag
        return carry

    lax.fori_loop(0, BLOCK // 8, products, 0)
    convolved = jnp.dot(
        inverse_ref[...], product_ref[...].astype(jnp.bfloat16), preferred_element_type=jnp.float32
    )
    for b in range(per):
        at = slice(b * BLOCK, (b + 1) * BLOCK)
        total = convolved[:, b * LANES : (b + 1) * LANES] + skip_ref[...] * mixed_ref[at, :]
        out_ref[at, :] = (query_ref[at, :] * total).astype(jnp.bfloat16)


EARLY = ((), (0,), (1,), (2,))
LATE = ((0, 1), (1, 2), (0, 2), (0, 1, 2))


def body(tokens, in_weight, short_weight, filter_taps, skip_gain):
    rows = tokens.shape[0]
    side = lax.axis_index("seq")
    place = jnp.stack([lax.axis_index("chan"), side]).astype(jnp.int32)
    precise, forward, inverse = odd_tables()
    held = tokens[None]
    x, y, z = (exchange(held, 0, k) for k in range(3))
    xy, yz, zx = exchange(y, 0, 0), exchange(z, 0, 1), exchange(x, 0, 2)
    early = join([held, x, y, z], xy, yz, zx, first=pltpu.HBM)
    weights = pack(place, in_weight, lax.ppermute(in_weight, "seq", SWAP))
    other_taps = lax.ppermute(filter_taps, "seq", SWAP)
    lag = pl.pallas_call(
        lag_kernel,
        out_shape=jax.ShapeDtypeStruct((2 * BLOCK, 2 * rows // BLOCK * LANES), jnp.float32),
        compiler_params=pltpu.CompilerParams(vmem_limit_bytes=16 << 20),
    )(jnp.where(side == 0, filter_taps, other_taps), jnp.where(side == 0, other_taps, filter_taps), precise)
    late = join([xy, yz, zx, exchange(yz, 0, 0)], weights, lag)

    def at(near, far):
        return tuple((n, far) for n in near)

    acc = project(place, [early, late], [at(EARLY, ()), at(LATE, ())], weights, None, False)
    firsts = [[exchange(h, 1, k) for k in range(3)] for h in (early, late)]
    every = (0, 1, 2)
    second0 = [exchange(after(firsts[0][(k + 1) % 3], acc), 1, k) for k in range(3)]
    acc = project(place, firsts[0], [at(EARLY, (k,)) for k in range(3)], weights, acc, False)
    second1 = [exchange(after(firsts[1][(k + 1) % 3], acc), 1, k) for k in range(3)]
    acc = project(place, firsts[1], [at(LATE, (k,)) for k in range(3)], weights, acc, False)
    pairs = ((0, 1), (1, 2), (0, 2))
    thirds = [exchange(after(second0[1], acc), 1, 0)]
    acc = project(place, second0, [at(EARLY, p) for p in pairs], weights, acc, False)
    thirds += [exchange(after(second1[0], acc), 1, 2)]
    names = [at(LATE, p) for p in pairs]
    acc = project(place, [*second1, thirds[0]], [*names, at(EARLY, every)], weights, acc, False)
    projected = [project(place, thirds[1:], [at(LATE, every)], weights, acc, True)]
    before = [lax.ppermute(p, "seq", [(0, 1)]) for p in projected]
    per = rows // BLOCK
    return pl.pallas_call(
        functools.partial(mix_kernel, parts=len(projected)),
        out_shape=jax.ShapeDtypeStruct((rows, LANES), jnp.bfloat16),
        scratch_shapes=[
            pltpu.VMEM((rows + 8, 3 * LANES), jnp.float32),
            pltpu.VMEM((rows + 8, 3 * LANES), jnp.float32),
            pltpu.VMEM((rows, LANES), jnp.float32),
            pltpu.VMEM((rows, LANES), jnp.float32),
            pltpu.VMEM((2 * BLOCK, 2 * per * LANES), jnp.float32),
            pltpu.VMEM((2 * BLOCK, per * LANES), jnp.float32),
        ],
        compiler_params=pltpu.CompilerParams(vmem_limit_bytes=16 << 20),
    )(*projected, *before, lag, short_weight, skip_gain.reshape(1, LANES), forward, inverse)


def solution(mesh):
    in_specs = (
        P("seq", "chan"),
        P(None, "seq", "chan"),
        P(None, None, "chan"),
        P("seq", "chan"),
        P("chan"),
    )
    out_specs = P("seq", "chan")
    return jax.shard_map(body, mesh=mesh, in_specs=in_specs, out_specs=out_specs, check_vma=False)
```

```python
import functools
import math

import jax
import jax.numpy as jnp
import ml_dtypes
import numpy as np
from jax import lax
from jax.experimental import pallas as pl
from jax.experimental.pallas import tpu as pltpu
from jax.sharding import PartitionSpec as P

BLOCK = 256
LANES = 128
SWAP = [(0, 1), (1, 0)]


def odd_tables():
    size = 2 * BLOCK
    angle = math.pi / size * (2 * np.arange(BLOCK)[:, None] + 1) * np.arange(BLOCK)[None, :]
    forward = np.concatenate([np.cos(angle), -np.sin(angle)])

    def parts(table):
        high = table.astype(ml_dtypes.bfloat16)
        low = (table - high.astype(np.float64)).astype(ml_dtypes.bfloat16)
        return jnp.asarray(np.concatenate([high, high, low], axis=1))

    inverse = forward.T * (2.0 / size)
    return parts(forward), jnp.asarray(forward.astype(ml_dtypes.bfloat16)), jnp.asarray(inverse.astype(ml_dtypes.bfloat16))


def split_rows(x):
    high = x.astype(jnp.bfloat16)
    low = (x - high.astype(jnp.float32)).astype(jnp.bfloat16)
    return jnp.concatenate([high, low, high], axis=0)


def lag_kernel(low_ref, high_ref, table_ref, out_ref):
    per = low_ref.shape[0] // BLOCK
    pieces = [low_ref[b * BLOCK : (b + 1) * BLOCK, :] for b in range(per)]
    pieces += [high_ref[b * BLOCK : (b + 1) * BLOCK, :] for b in range(per)]
    spectrum = jnp.dot(
        table_ref[...], split_rows(jnp.concatenate(pieces, axis=1)), preferred_element_type=jnp.float32
    )
    real, imag = spectrum[:BLOCK], spectrum[BLOCK:]
    parity = lax.broadcasted_iota(jnp.int32, (BLOCK, LANES), 0) % 2
    sign = jnp.where(parity == 0, 1.0, -1.0).astype(jnp.float32)
    for m in range(2 * per):
        at = slice(m * LANES, (m + 1) * LANES)
        if m == 0:
            out_ref[:BLOCK, at] = real[:, at]
            out_ref[BLOCK:, at] = imag[:, at]
        else:
            before = slice((m - 1) * LANES, m * LANES)
            out_ref[:BLOCK, at] = real[:, at] - sign * imag[:, before]
            out_ref[BLOCK:, at] = imag[:, at] + sign * real[:, before]


SHIFTS = (0, 2, 4)
STEPS = ((1, 3), (3, 1))


def masks_of(near, far, core):
    return sum(STEPS[0][core] << SHIFTS[k] for k in near) ^ sum(STEPS[1][core] << SHIFTS[k] for k in far)


def project_kernel(place_ref, *refs, sources, start):
    count = len(sources)
    pieces, weight_ref = refs[:count], refs[count]
    out_ref = refs[-1]
    chip, side = place_ref[0], place_ref[1]
    lefts, rights = [], []
    for piece_ref, source in zip(pieces, sources, strict=True):
        for b, (near, far) in enumerate(source):
            at = chip ^ jnp.where(side == 0, masks_of(near, far, 0), masks_of(near, far, 1))
            rights.append(weight_ref[at])
            lefts.append(piece_ref[b])
    total = jnp.dot(
        jnp.concatenate(lefts, axis=1), jnp.concatenate(rights, axis=0), preferred_element_type=jnp.float32
    )
    if not start:
        total += refs[count + 1][...]
    out_ref[...] = total.astype(out_ref.dtype)


def pack_kernel(place_ref, own_ref, other_ref, out_ref, sems):
    side = place_ref[1]
    half = own_ref.shape[1]
    copies = []
    for n, (ref, at) in enumerate(((own_ref, side), (other_ref, 1 - side))):
        for p in range(3):
            to = out_ref.at[pl.ds(at * half, half), :, pl.ds(p * LANES, LANES)]
            copies.append(pltpu.make_async_copy(ref.at[p], to, sems.at[3 * n + p]))
    for copy in copies:
        copy.start()
    for copy in copies:
        copy.wait()


def pack(place, own, other):
    own, other = (w.reshape(3, -1, LANES, LANES) for w in (own, other))
    return pl.pallas_call(
        pack_kernel,
        out_shape=jax.ShapeDtypeStruct((2 * own.shape[1], LANES, 3 * LANES), jnp.bfloat16),
        in_specs=[pl.BlockSpec(memory_space=pltpu.SMEM)] + [pl.BlockSpec(memory_space=pltpu.HBM)] * 2,
        out_specs=pl.BlockSpec(memory_space=pltpu.VMEM),
        scratch_shapes=[pltpu.SemaphoreType.DMA((6,))],
        compiler_params=pltpu.CompilerParams(vmem_limit_bytes=14 << 20),
    )(place, own, other)


def join_kernel(*refs, count):
    out_ref, sems = refs[-2:]
    copies = [pltpu.make_async_copy(refs[n], out_ref.at[pl.ds(n, 1)], sems.at[n]) for n in range(count)]
    for copy in copies:
        copy.start()
    for copy in copies:
        copy.wait()


def join(blocks, *earlier, first=pl.ANY):
    args = [*blocks, *earlier]
    return pl.pallas_call(
        functools.partial(join_kernel, count=len(blocks)),
        out_shape=jax.ShapeDtypeStruct((len(blocks), *blocks[0].shape[1:]), blocks[0].dtype),
        in_specs=[pl.BlockSpec(memory_space=first)] + [pl.BlockSpec(memory_space=pl.ANY)] * (len(args) - 1),
        out_specs=pl.BlockSpec(memory_space=pltpu.VMEM),
        scratch_shapes=[pltpu.SemaphoreType.DMA((len(blocks),))],
        compiler_params=pltpu.CompilerParams(vmem_limit_bytes=8 << 20),
    )(*args)


def project(place, pieces, sources, weights, before, final):
    rows = pieces[0].shape[1]
    args = [*pieces, weights] + ([] if before is None else [before])
    return pl.pallas_call(
        functools.partial(project_kernel, sources=sources, start=before is None),
        out_shape=jax.ShapeDtypeStruct((rows, 3 * LANES), jnp.bfloat16 if final else jnp.float32),
        in_specs=[pl.BlockSpec(memory_space=pltpu.SMEM)] + [pl.BlockSpec(memory_space=pltpu.VMEM)] * len(args),
        out_specs=pl.BlockSpec(memory_space=pltpu.VMEM),
        compiler_params=pltpu.CompilerParams(vmem_limit_bytes=14 << 20),
        cost_estimate=pl.CostEstimate(
            flops=4 * rows * 3 * LANES * LANES * sum(p.shape[0] for p in pieces),
            transcendentals=0,
            bytes_accessed=8 << 20,
        ),
    )(place, *args)


def after(block, earlier):
    return lax.optimization_barrier((block, earlier))[0]


def exchange(block, turn, axis):
    route = []
    for chip in range(64):
        for side in range(2):
            to = chip ^ (STEPS[turn][side] << SHIFTS[axis])
            route.append((chip * 2 + side, to * 2 + side))
    return lax.ppermute(block, ("chan", "seq"), route)


def mix_kernel(
    *refs, parts
):
    own_refs, before_refs = refs[:parts], refs[parts : 2 * parts]
    lag_ref, short_ref, skip_ref, forward_ref, inverse_ref, out_ref = refs[2 * parts : 2 * parts + 6]
    wide_ref, past_ref, query_ref, mixed_ref, spectrum_ref, product_ref = refs[2 * parts + 6 :]
    rows = out_ref.shape[0]
    per = rows // BLOCK
    past_ref[0:8, :] = jnp.zeros((8, 3 * LANES), jnp.float32)
    at = 8
    for own_ref, before_ref in zip(own_refs, before_refs, strict=True):
        past_ref[at : at + own_ref.shape[0], :] = before_ref[...].astype(jnp.float32)
        wide_ref[at : at + own_ref.shape[0], :] = own_ref[...].astype(jnp.float32)
        at += own_ref.shape[0]
    wide_ref[0:8, :] = past_ref[rows:, :]

    def tapped(ref, block, which):
        at = slice(which * LANES, (which + 1) * LANES)
        start = 8 + block * BLOCK
        total = short_ref[0, which : which + 1, :] * ref[start : start + BLOCK, at]
        total += short_ref[1, which : which + 1, :] * ref[start - 1 : start - 1 + BLOCK, at]
        total += short_ref[2, which : which + 1, :] * ref[start - 2 : start - 2 + BLOCK, at]
        return total

    pieces = [tapped(past_ref, b, 1) * tapped(past_ref, b, 2) for b in range(per)]
    for b in range(per):
        mixed = tapped(wide_ref, b, 1) * tapped(wide_ref, b, 2)
        mixed_ref[b * BLOCK : (b + 1) * BLOCK, :] = mixed
        query_ref[b * BLOCK : (b + 1) * BLOCK, :] = tapped(wide_ref, b, 0)
        pieces.append(mixed)
    spectrum_ref[...] = jnp.dot(
        forward_ref[...], jnp.concatenate(pieces, axis=1).astype(jnp.bfloat16),
        preferred_element_type=jnp.float32,
    )

    def products(group, carry):
        at_real = pl.ds(pl.multiple_of(group * 8, 8), 8)
        at_imag = pl.ds(pl.multiple_of(BLOCK + group * 8, 8), 8)
        lanes = [slice(j * LANES, (j + 1) * LANES) for j in range(2 * per)]
        signal = [(spectrum_ref[at_real, at], spectrum_ref[at_imag, at]) for at in lanes]
        lag = [(lag_ref[at_real, at], lag_ref[at_imag, at]) for at in lanes]
        for i in range(per):
            real = imag = None
            for j in range(per + i + 1):
                xr, xi = signal[j]
                hr, hi = lag[per + i - j]
                pr, pi = xr * hr - xi * hi, xr * hi + xi * hr
                real, imag = (pr, pi) if real is None else (real + pr, imag + pi)
            product_ref[at_real, i * LANES : (i + 1) * LANES] = real
            product_ref[at_imag, i * LANES : (i + 1) * LANES] = imag
        return carry

    lax.fori_loop(0, BLOCK // 8, products, 0)
    convolved = jnp.dot(
        inverse_ref[...], product_ref[...].astype(jnp.bfloat16), preferred_element_type=jnp.float32
    )
    for b in range(per):
        at = slice(b * BLOCK, (b + 1) * BLOCK)
        total = convolved[:, b * LANES : (b + 1) * LANES] + skip_ref[...] * mixed_ref[at, :]
        out_ref[at, :] = (query_ref[at, :] * total).astype(jnp.bfloat16)


EARLY = ((), (0,), (1,), (2,))
LATE = ((0, 1), (1, 2), (0, 2), (0, 1, 2))


def body(tokens, in_weight, short_weight, filter_taps, skip_gain):
    rows = tokens.shape[0]
    side = lax.axis_index("seq")
    place = jnp.stack([lax.axis_index("chan"), side]).astype(jnp.int32)
    precise, forward, inverse = odd_tables()
    held = tokens[None]
    x, y, z = (exchange(held, 0, k) for k in range(3))
    xy, yz, zx = exchange(y, 0, 0), exchange(z, 0, 1), exchange(x, 0, 2)
    early = join([held, x, y, z], xy, yz, zx, first=pltpu.HBM)
    weights = pack(place, in_weight, lax.ppermute(in_weight, "seq", SWAP))
    other_taps = lax.ppermute(filter_taps, "seq", SWAP)
    lag = pl.pallas_call(
        lag_kernel,
        out_shape=jax.ShapeDtypeStruct((2 * BLOCK, 2 * rows // BLOCK * LANES), jnp.float32),
        compiler_params=pltpu.CompilerParams(vmem_limit_bytes=16 << 20),
    )(jnp.where(side == 0, filter_taps, other_taps), jnp.where(side == 0, other_taps, filter_taps), precise)
    late = join([xy, yz, zx, exchange(yz, 0, 0)], weights, lag)

    def at(near, far):
        return tuple((n, far) for n in near)

    acc = project(place, [early, late], [at(EARLY, ()), at(LATE, ())], weights, None, False)
    firsts = [[exchange(h, 1, k) for k in range(3)] for h in (early, late)]
    every = (0, 1, 2)
    second0 = [exchange(after(firsts[0][(k + 1) % 3], acc), 1, k) for k in range(3)]
    acc = project(place, firsts[0], [at(EARLY, (k,)) for k in range(3)], weights, acc, False)
    second1 = [exchange(after(firsts[1][(k + 1) % 3], acc), 1, k) for k in range(3)]
    acc = project(place, firsts[1], [at(LATE, (k,)) for k in range(3)], weights, acc, False)
    pairs = ((0, 1), (1, 2), (0, 2))
    thirds = [exchange(after(second0[1], acc), 1, 0)]
    acc = project(place, second0, [at(EARLY, p) for p in pairs], weights, acc, False)
    thirds += [exchange(after(second1[0], acc)[:3], 1, 2), exchange(after(second1[2], acc)[3:], 1, 1)]
    names = [at(LATE, p) for p in pairs]
    acc = project(place, second1, names, weights, acc, False)
    names = [at(EARLY, every), at(LATE[:3], every), at(LATE[3:], every)]
    projected = [project(place, thirds, names, weights, acc, True)]
    before = [lax.ppermute(p, "seq", [(0, 1)]) for p in projected]
    per = rows // BLOCK
    return pl.pallas_call(
        functools.partial(mix_kernel, parts=len(projected)),
        out_shape=jax.ShapeDtypeStruct((rows, LANES), jnp.bfloat16),
        scratch_shapes=[
            pltpu.VMEM((rows + 8, 3 * LANES), jnp.float32),
            pltpu.VMEM((rows + 8, 3 * LANES), jnp.float32),
            pltpu.VMEM((rows, LANES), jnp.float32),
            pltpu.VMEM((rows, LANES), jnp.float32),
            pltpu.VMEM((2 * BLOCK, 2 * per * LANES), jnp.float32),
            pltpu.VMEM((2 * BLOCK, per * LANES), jnp.float32),
        ],
        compiler_params=pltpu.CompilerParams(vmem_limit_bytes=16 << 20),
    )(*projected, *before, lag, short_weight, skip_gain.reshape(1, LANES), forward, inverse)


def solution(mesh):
    in_specs = (
        P("seq", "chan"),
        P(None, "seq", "chan"),
        P(None, None, "chan"),
        P("seq", "chan"),
        P("chan"),
    )
    out_specs = P("seq", "chan")
    return jax.shard_map(body, mesh=mesh, in_specs=in_specs, out_specs=out_specs, check_vma=False)
```

```python
import functools
import math

import jax
import jax.numpy as jnp
import ml_dtypes
import numpy as np
from jax import lax
from jax.experimental import pallas as pl
from jax.experimental.pallas import tpu as pltpu
from jax.sharding import PartitionSpec as P

BLOCK = 256
LANES = 128
SWAP = [(0, 1), (1, 0)]


def odd_tables():
    size = 2 * BLOCK
    angle = math.pi / size * (2 * np.arange(BLOCK)[:, None] + 1) * np.arange(BLOCK)[None, :]
    forward = np.concatenate([np.cos(angle), -np.sin(angle)])

    def parts(table):
        high = table.astype(ml_dtypes.bfloat16)
        low = (table - high.astype(np.float64)).astype(ml_dtypes.bfloat16)
        return jnp.asarray(np.concatenate([high, high, low], axis=1))

    inverse = forward.T * (2.0 / size)
    return parts(forward), jnp.asarray(forward.astype(ml_dtypes.bfloat16)), jnp.asarray(inverse.astype(ml_dtypes.bfloat16))


def split_rows(x):
    high = x.astype(jnp.bfloat16)
    low = (x - high.astype(jnp.float32)).astype(jnp.bfloat16)
    return jnp.concatenate([high, low, high], axis=0)


def lag_kernel(low_ref, high_ref, table_ref, out_ref):
    per = low_ref.shape[0] // BLOCK
    pieces = [low_ref[b * BLOCK : (b + 1) * BLOCK, :] for b in range(per)]
    pieces += [high_ref[b * BLOCK : (b + 1) * BLOCK, :] for b in range(per)]
    spectrum = jnp.dot(
        table_ref[...], split_rows(jnp.concatenate(pieces, axis=1)), preferred_element_type=jnp.float32
    )
    real, imag = spectrum[:BLOCK], spectrum[BLOCK:]
    parity = lax.broadcasted_iota(jnp.int32, (BLOCK, LANES), 0) % 2
    sign = jnp.where(parity == 0, 1.0, -1.0).astype(jnp.float32)
    for m in range(2 * per):
        at = slice(m * LANES, (m + 1) * LANES)
        if m == 0:
            out_ref[:BLOCK, at] = real[:, at]
            out_ref[BLOCK:, at] = imag[:, at]
        else:
            before = slice((m - 1) * LANES, m * LANES)
            out_ref[:BLOCK, at] = real[:, at] - sign * imag[:, before]
            out_ref[BLOCK:, at] = imag[:, at] + sign * real[:, before]


SHIFTS = (0, 2, 4)
STEPS = ((1, 3), (3, 1))


def masks_of(near, far, core):
    return sum(STEPS[0][core] << SHIFTS[k] for k in near) ^ sum(STEPS[1][core] << SHIFTS[k] for k in far)


def project_kernel(place_ref, *refs, sources, start):
    count = len(sources)
    pieces, weight_ref = refs[:count], refs[count]
    out_ref = refs[-1]
    chip, side = place_ref[0], place_ref[1]
    lefts, rights = [], []
    for piece_ref, source in zip(pieces, sources, strict=True):
        for b, (near, far) in enumerate(source):
            at = chip ^ jnp.where(side == 0, masks_of(near, far, 0), masks_of(near, far, 1))
            rights.append(weight_ref[at])
            lefts.append(piece_ref[b])
    total = jnp.dot(
        jnp.concatenate(lefts, axis=1), jnp.concatenate(rights, axis=0), preferred_element_type=jnp.float32
    )
    if not start:
        total += refs[count + 1][...]
    out_ref[...] = total.astype(out_ref.dtype)


def pack_kernel(place_ref, own_ref, other_ref, out_ref, sems):
    side = place_ref[1]
    half = own_ref.shape[1]
    copies = []
    for n, (ref, at) in enumerate(((own_ref, side), (other_ref, 1 - side))):
        for p in range(3):
            to = out_ref.at[pl.ds(at * half, half), :, pl.ds(p * LANES, LANES)]
            copies.append(pltpu.make_async_copy(ref.at[p], to, sems.at[3 * n + p]))
    for copy in copies:
        copy.start()
    for copy in copies:
        copy.wait()


def pack(place, own, other):
    own, other = (w.reshape(3, -1, LANES, LANES) for w in (own, other))
    return pl.pallas_call(
        pack_kernel,
        out_shape=jax.ShapeDtypeStruct((2 * own.shape[1], LANES, 3 * LANES), jnp.bfloat16),
        in_specs=[pl.BlockSpec(memory_space=pltpu.SMEM)] + [pl.BlockSpec(memory_space=pltpu.HBM)] * 2,
        out_specs=pl.BlockSpec(memory_space=pltpu.VMEM),
        scratch_shapes=[pltpu.SemaphoreType.DMA((6,))],
        compiler_params=pltpu.CompilerParams(vmem_limit_bytes=14 << 20),
    )(place, own, other)


def join_kernel(*refs, count):
    out_ref, sems = refs[-2:]
    copies = [pltpu.make_async_copy(refs[n], out_ref.at[pl.ds(n, 1)], sems.at[n]) for n in range(count)]
    for copy in copies:
        copy.start()
    for copy in copies:
        copy.wait()


def join(blocks, *earlier, first=pl.ANY):
    args = [*blocks, *earlier]
    return pl.pallas_call(
        functools.partial(join_kernel, count=len(blocks)),
        out_shape=jax.ShapeDtypeStruct((len(blocks), *blocks[0].shape[1:]), blocks[0].dtype),
        in_specs=[pl.BlockSpec(memory_space=first)] + [pl.BlockSpec(memory_space=pl.ANY)] * (len(args) - 1),
        out_specs=pl.BlockSpec(memory_space=pltpu.VMEM),
        scratch_shapes=[pltpu.SemaphoreType.DMA((len(blocks),))],
        compiler_params=pltpu.CompilerParams(vmem_limit_bytes=8 << 20),
    )(*args)


def project(place, pieces, sources, weights, before, final):
    rows = pieces[0].shape[1]
    args = [*pieces, weights] + ([] if before is None else [before])
    return pl.pallas_call(
        functools.partial(project_kernel, sources=sources, start=before is None),
        out_shape=jax.ShapeDtypeStruct((rows, 3 * LANES), jnp.bfloat16 if final else jnp.float32),
        in_specs=[pl.BlockSpec(memory_space=pltpu.SMEM)] + [pl.BlockSpec(memory_space=pltpu.VMEM)] * len(args),
        out_specs=pl.BlockSpec(memory_space=pltpu.VMEM),
        compiler_params=pltpu.CompilerParams(vmem_limit_bytes=14 << 20),
        cost_estimate=pl.CostEstimate(
            flops=4 * rows * 3 * LANES * LANES * sum(p.shape[0] for p in pieces),
            transcendentals=0,
            bytes_accessed=8 << 20,
        ),
    )(place, *args)


def after(block, earlier):
    return lax.optimization_barrier((block, earlier))[0]


def exchange(block, turn, axis):
    route = []
    for chip in range(64):
        for side in range(2):
            to = chip ^ (STEPS[turn][side] << SHIFTS[axis])
            route.append((chip * 2 + side, to * 2 + side))
    return lax.ppermute(block, ("chan", "seq"), route)


def mix_kernel(
    *refs, parts
):
    own_refs, before_refs = refs[:parts], refs[parts : 2 * parts]
    lag_ref, short_ref, skip_ref, forward_ref, inverse_ref, out_ref = refs[2 * parts : 2 * parts + 6]
    wide_ref, past_ref, query_ref, mixed_ref, spectrum_ref, product_ref = refs[2 * parts + 6 :]
    rows = out_ref.shape[0]
    per = rows // BLOCK
    past_ref[0:8, :] = jnp.zeros((8, 3 * LANES), jnp.float32)
    at = 8
    for own_ref, before_ref in zip(own_refs, before_refs, strict=True):
        past_ref[at : at + own_ref.shape[0], :] = before_ref[...].astype(jnp.float32)
        wide_ref[at : at + own_ref.shape[0], :] = own_ref[...].astype(jnp.float32)
        at += own_ref.shape[0]
    wide_ref[0:8, :] = past_ref[rows:, :]

    def tapped(ref, block, which):
        at = slice(which * LANES, (which + 1) * LANES)
        start = 8 + block * BLOCK
        total = short_ref[0, which : which + 1, :] * ref[start : start + BLOCK, at]
        total += short_ref[1, which : which + 1, :] * ref[start - 1 : start - 1 + BLOCK, at]
        total += short_ref[2, which : which + 1, :] * ref[start - 2 : start - 2 + BLOCK, at]
        return total

    pieces = [tapped(past_ref, b, 1) * tapped(past_ref, b, 2) for b in range(per)]
    for b in range(per):
        mixed = tapped(wide_ref, b, 1) * tapped(wide_ref, b, 2)
        mixed_ref[b * BLOCK : (b + 1) * BLOCK, :] = mixed
        query_ref[b * BLOCK : (b + 1) * BLOCK, :] = tapped(wide_ref, b, 0)
        pieces.append(mixed)
    spectrum_ref[...] = jnp.dot(
        forward_ref[...], jnp.concatenate(pieces, axis=1).astype(jnp.bfloat16),
        preferred_element_type=jnp.float32,
    )

    def products(group, carry):
        at_real = pl.ds(pl.multiple_of(group * 8, 8), 8)
        at_imag = pl.ds(pl.multiple_of(BLOCK + group * 8, 8), 8)
        lanes = [slice(j * LANES, (j + 1) * LANES) for j in range(2 * per)]
        signal = [(spectrum_ref[at_real, at], spectrum_ref[at_imag, at]) for at in lanes]
        lag = [(lag_ref[at_real, at], lag_ref[at_imag, at]) for at in lanes]
        for i in range(per):
            real = imag = None
            for j in range(per + i + 1):
                xr, xi = signal[j]
                hr, hi = lag[per + i - j]
                pr, pi = xr * hr - xi * hi, xr * hi + xi * hr
                real, imag = (pr, pi) if real is None else (real + pr, imag + pi)
            product_ref[at_real, i * LANES : (i + 1) * LANES] = real
            product_ref[at_imag, i * LANES : (i + 1) * LANES] = imag
        return carry

    lax.fori_loop(0, BLOCK // 8, products, 0, unroll=2)
    convolved = jnp.dot(
        inverse_ref[...], product_ref[...].astype(jnp.bfloat16), preferred_element_type=jnp.float32
    )
    for b in range(per):
        at = slice(b * BLOCK, (b + 1) * BLOCK)
        total = convolved[:, b * LANES : (b + 1) * LANES] + skip_ref[...] * mixed_ref[at, :]
        out_ref[at, :] = (query_ref[at, :] * total).astype(jnp.bfloat16)


EARLY = ((), (0,), (1,), (2,))
LATE = ((0, 1), (1, 2), (0, 2), (0, 1, 2))


def body(tokens, in_weight, short_weight, filter_taps, skip_gain):
    rows = tokens.shape[0]
    side = lax.axis_index("seq")
    place = jnp.stack([lax.axis_index("chan"), side]).astype(jnp.int32)
    precise, forward, inverse = odd_tables()
    held = tokens[None]
    x, y, z = (exchange(held, 0, k) for k in range(3))
    xy, yz, zx = exchange(y, 0, 0), exchange(z, 0, 1), exchange(x, 0, 2)
    early = join([held, x, y, z], xy, yz, first=pltpu.HBM)
    weights = pack(place, in_weight, lax.ppermute(in_weight, "seq", SWAP))
    other_taps = lax.ppermute(filter_taps, "seq", SWAP)
    lag = pl.pallas_call(
        lag_kernel,
        out_shape=jax.ShapeDtypeStruct((2 * BLOCK, 2 * rows // BLOCK * LANES), jnp.float32),
        compiler_params=pltpu.CompilerParams(vmem_limit_bytes=16 << 20),
    )(jnp.where(side == 0, filter_taps, other_taps), jnp.where(side == 0, other_taps, filter_taps), precise)
    late = join([xy, yz, zx, exchange(yz, 0, 0)], weights, lag)

    def at(near, far):
        return tuple((n, far) for n in near)

    acc = project(place, [early, late], [at(EARLY, ()), at(LATE, ())], weights, None, False)
    firsts = [[exchange(h, 1, k) for k in range(3)] for h in (early, late)]
    every = (0, 1, 2)
    second0 = [exchange(after(firsts[0][(k + 1) % 3], acc), 1, k) for k in range(3)]
    acc = project(place, firsts[0], [at(EARLY, (k,)) for k in range(3)], weights, acc, False)
    second1 = [exchange(after(firsts[1][(k + 1) % 3], acc), 1, k) for k in range(3)]
    acc = project(place, firsts[1], [at(LATE, (k,)) for k in range(3)], weights, acc, False)
    pairs = ((0, 1), (1, 2), (0, 2))
    thirds = [exchange(after(second0[1], acc), 1, 0)]
    acc = project(place, second0, [at(EARLY, p) for p in pairs], weights, acc, False)
    thirds += [exchange(after(second1[0], acc)[:3], 1, 2), exchange(after(second1[2], acc)[3:], 1, 1)]
    names = [at(LATE, p) for p in pairs]
    acc = project(place, second1, names, weights, acc, False)
    names = [at(EARLY, every), at(LATE[:3], every), at(LATE[3:], every)]
    projected = [project(place, thirds, names, weights, acc, True)]
    before = [lax.ppermute(p, "seq", [(0, 1)]) for p in projected]
    per = rows // BLOCK
    return pl.pallas_call(
        functools.partial(mix_kernel, parts=len(projected)),
        out_shape=jax.ShapeDtypeStruct((rows, LANES), jnp.bfloat16),
        scratch_shapes=[
            pltpu.VMEM((rows + 8, 3 * LANES), jnp.float32),
            pltpu.VMEM((rows + 8, 3 * LANES), jnp.float32),
            pltpu.VMEM((rows, LANES), jnp.float32),
            pltpu.VMEM((rows, LANES), jnp.float32),
            pltpu.VMEM((2 * BLOCK, 2 * per * LANES), jnp.float32),
            pltpu.VMEM((2 * BLOCK, per * LANES), jnp.float32),
        ],
        compiler_params=pltpu.CompilerParams(vmem_limit_bytes=16 << 20),
    )(*projected, *before, lag, short_weight, skip_gain.reshape(1, LANES), forward, inverse)


def solution(mesh):
    in_specs = (
        P("seq", "chan"),
        P(None, "seq", "chan"),
        P(None, None, "chan"),
        P("seq", "chan"),
        P("chan"),
    )
    out_specs = P("seq", "chan")
    return jax.shard_map(body, mesh=mesh, in_specs=in_specs, out_specs=out_specs, check_vma=False)
```

```python
import functools
import math

import jax
import jax.numpy as jnp
import ml_dtypes
import numpy as np
from jax import lax
from jax.experimental import pallas as pl
from jax.experimental.pallas import tpu as pltpu
from jax.sharding import PartitionSpec as P

BLOCK = 256
LANES = 128
SWAP = [(0, 1), (1, 0)]


def odd_tables():
    size = 2 * BLOCK
    angle = math.pi / size * (2 * np.arange(BLOCK)[:, None] + 1) * np.arange(BLOCK)[None, :]
    forward = np.concatenate([np.cos(angle), -np.sin(angle)])

    def parts(table):
        high = table.astype(ml_dtypes.bfloat16)
        low = (table - high.astype(np.float64)).astype(ml_dtypes.bfloat16)
        return jnp.asarray(np.concatenate([high, high, low], axis=1))

    inverse = forward.T * (2.0 / size)
    return parts(forward), jnp.asarray(forward.astype(ml_dtypes.bfloat16)), jnp.asarray(inverse.astype(ml_dtypes.bfloat16))


def split_rows(x):
    high = x.astype(jnp.bfloat16)
    low = (x - high.astype(jnp.float32)).astype(jnp.bfloat16)
    return jnp.concatenate([high, low, high], axis=0)


def lag_kernel(low_ref, high_ref, table_ref, out_ref):
    per = low_ref.shape[0] // BLOCK
    pieces = [low_ref[b * BLOCK : (b + 1) * BLOCK, :] for b in range(per)]
    pieces += [high_ref[b * BLOCK : (b + 1) * BLOCK, :] for b in range(per)]
    spectrum = jnp.dot(
        table_ref[...], split_rows(jnp.concatenate(pieces, axis=1)), preferred_element_type=jnp.float32
    )
    real, imag = spectrum[:BLOCK], spectrum[BLOCK:]
    parity = lax.broadcasted_iota(jnp.int32, (BLOCK, LANES), 0) % 2
    sign = jnp.where(parity == 0, 1.0, -1.0).astype(jnp.float32)
    for m in range(2 * per):
        at = slice(m * LANES, (m + 1) * LANES)
        if m == 0:
            out_ref[:BLOCK, at] = real[:, at]
            out_ref[BLOCK:, at] = imag[:, at]
        else:
            before = slice((m - 1) * LANES, m * LANES)
            out_ref[:BLOCK, at] = real[:, at] - sign * imag[:, before]
            out_ref[BLOCK:, at] = imag[:, at] + sign * real[:, before]


SHIFTS = (0, 2, 4)
STEPS = ((1, 3), (3, 1))


def masks_of(near, far, core):
    return sum(STEPS[0][core] << SHIFTS[k] for k in near) ^ sum(STEPS[1][core] << SHIFTS[k] for k in far)


def project_kernel(place_ref, *refs, sources, start):
    count = len(sources)
    pieces, weight_ref = refs[:count], refs[count]
    out_ref = refs[-1]
    chip, side = place_ref[0], place_ref[1]
    lefts, rights = [], []
    for piece_ref, source in zip(pieces, sources, strict=True):
        for b, (near, far) in enumerate(source):
            at = chip ^ jnp.where(side == 0, masks_of(near, far, 0), masks_of(near, far, 1))
            rights.append(weight_ref[at])
            lefts.append(piece_ref[b])
    total = jnp.dot(
        jnp.concatenate(lefts, axis=1), jnp.concatenate(rights, axis=0), preferred_element_type=jnp.float32
    )
    if not start:
        total += refs[count + 1][...]
    out_ref[...] = total.astype(out_ref.dtype)


def pack_kernel(place_ref, own_ref, other_ref, out_ref, sems):
    side = place_ref[1]
    half = own_ref.shape[1]
    copies = []
    for n, (ref, at) in enumerate(((own_ref, side), (other_ref, 1 - side))):
        for p in range(3):
            to = out_ref.at[pl.ds(at * half, half), :, pl.ds(p * LANES, LANES)]
            copies.append(pltpu.make_async_copy(ref.at[p], to, sems.at[3 * n + p]))
    for copy in copies:
        copy.start()
    for copy in copies:
        copy.wait()


def pack(place, own, other):
    own, other = (w.reshape(3, -1, LANES, LANES) for w in (own, other))
    return pl.pallas_call(
        pack_kernel,
        out_shape=jax.ShapeDtypeStruct((2 * own.shape[1], LANES, 3 * LANES), jnp.bfloat16),
        in_specs=[pl.BlockSpec(memory_space=pltpu.SMEM)] + [pl.BlockSpec(memory_space=pltpu.HBM)] * 2,
        out_specs=pl.BlockSpec(memory_space=pltpu.VMEM),
        scratch_shapes=[pltpu.SemaphoreType.DMA((6,))],
        compiler_params=pltpu.CompilerParams(vmem_limit_bytes=14 << 20),
    )(place, own, other)


def join_kernel(*refs, count):
    out_ref, sems = refs[-2:]
    copies = [pltpu.make_async_copy(refs[n], out_ref.at[pl.ds(n, 1)], sems.at[n]) for n in range(count)]
    for copy in copies:
        copy.start()
    for copy in copies:
        copy.wait()


def join(blocks, *earlier, first=pl.ANY):
    args = [*blocks, *earlier]
    return pl.pallas_call(
        functools.partial(join_kernel, count=len(blocks)),
        out_shape=jax.ShapeDtypeStruct((len(blocks), *blocks[0].shape[1:]), blocks[0].dtype),
        in_specs=[pl.BlockSpec(memory_space=first)] + [pl.BlockSpec(memory_space=pl.ANY)] * (len(args) - 1),
        out_specs=pl.BlockSpec(memory_space=pltpu.VMEM),
        scratch_shapes=[pltpu.SemaphoreType.DMA((len(blocks),))],
        compiler_params=pltpu.CompilerParams(vmem_limit_bytes=8 << 20),
    )(*args)


def project(place, pieces, sources, weights, before, final):
    rows = pieces[0].shape[1]
    args = [*pieces, weights] + ([] if before is None else [before])
    return pl.pallas_call(
        functools.partial(project_kernel, sources=sources, start=before is None),
        out_shape=jax.ShapeDtypeStruct((rows, 3 * LANES), jnp.bfloat16 if final else jnp.float32),
        in_specs=[pl.BlockSpec(memory_space=pltpu.SMEM)] + [pl.BlockSpec(memory_space=pltpu.VMEM)] * len(args),
        out_specs=pl.BlockSpec(memory_space=pltpu.VMEM),
        compiler_params=pltpu.CompilerParams(vmem_limit_bytes=14 << 20),
        cost_estimate=pl.CostEstimate(
            flops=4 * rows * 3 * LANES * LANES * sum(p.shape[0] for p in pieces),
            transcendentals=0,
            bytes_accessed=8 << 20,
        ),
    )(place, *args)


def after(block, earlier):
    return lax.optimization_barrier((block, earlier))[0]


def exchange(block, turn, axis):
    route = []
    for chip in range(64):
        for side in range(2):
            to = chip ^ (STEPS[turn][side] << SHIFTS[axis])
            route.append((chip * 2 + side, to * 2 + side))
    return lax.ppermute(block, ("chan", "seq"), route)


def mix_kernel(
    *refs, parts
):
    own_refs, before_refs = refs[:parts], refs[parts : 2 * parts]
    lag_ref, short_ref, skip_ref, forward_ref, inverse_ref, out_ref = refs[2 * parts : 2 * parts + 6]
    wide_ref, past_ref, query_ref, mixed_ref, spectrum_ref, product_ref = refs[2 * parts + 6 :]
    rows = out_ref.shape[0]
    per = rows // BLOCK
    past_ref[0:8, :] = jnp.zeros((8, 3 * LANES), jnp.float32)
    at = 8
    for own_ref, before_ref in zip(own_refs, before_refs, strict=True):
        past_ref[at : at + own_ref.shape[0], LANES:] = before_ref[:, LANES:].astype(jnp.float32)
        wide_ref[at : at + own_ref.shape[0], :] = own_ref[...].astype(jnp.float32)
        at += own_ref.shape[0]
    past_ref[rows - 8 :, :LANES] = before_refs[-1][before_refs[-1].shape[0] - 16 :, :LANES].astype(jnp.float32)
    wide_ref[0:8, :] = past_ref[rows:, :]

    def tapped(ref, block, which):
        at = slice(which * LANES, (which + 1) * LANES)
        start = 8 + block * BLOCK
        total = short_ref[0, which : which + 1, :] * ref[start : start + BLOCK, at]
        total += short_ref[1, which : which + 1, :] * ref[start - 1 : start - 1 + BLOCK, at]
        total += short_ref[2, which : which + 1, :] * ref[start - 2 : start - 2 + BLOCK, at]
        return total

    pieces = [tapped(past_ref, b, 1) * tapped(past_ref, b, 2) for b in range(per)]
    for b in range(per):
        mixed = tapped(wide_ref, b, 1) * tapped(wide_ref, b, 2)
        mixed_ref[b * BLOCK : (b + 1) * BLOCK, :] = mixed
        query_ref[b * BLOCK : (b + 1) * BLOCK, :] = tapped(wide_ref, b, 0)
        pieces.append(mixed)
    spectrum_ref[...] = jnp.dot(
        forward_ref[...], jnp.concatenate(pieces, axis=1).astype(jnp.bfloat16),
        preferred_element_type=jnp.float32,
    )

    def products(group, carry):
        at_real = pl.ds(pl.multiple_of(group * 8, 8), 8)
        at_imag = pl.ds(pl.multiple_of(BLOCK + group * 8, 8), 8)
        lanes = [slice(j * LANES, (j + 1) * LANES) for j in range(2 * per)]
        signal = [(spectrum_ref[at_real, at], spectrum_ref[at_imag, at]) for at in lanes]
        lag = [(lag_ref[at_real, at], lag_ref[at_imag, at]) for at in lanes]
        for i in range(per):
            real = imag = None
            for j in range(per + i + 1):
                xr, xi = signal[j]
                hr, hi = lag[per + i - j]
                pr, pi = xr * hr - xi * hi, xr * hi + xi * hr
                real, imag = (pr, pi) if real is None else (real + pr, imag + pi)
            product_ref[at_real, i * LANES : (i + 1) * LANES] = real
            product_ref[at_imag, i * LANES : (i + 1) * LANES] = imag
        return carry

    lax.fori_loop(0, BLOCK // 8, products, 0, unroll=2)
    convolved = jnp.dot(
        inverse_ref[...], product_ref[...].astype(jnp.bfloat16), preferred_element_type=jnp.float32
    )
    for b in range(per):
        at = slice(b * BLOCK, (b + 1) * BLOCK)
        total = convolved[:, b * LANES : (b + 1) * LANES] + skip_ref[...] * mixed_ref[at, :]
        out_ref[at, :] = (query_ref[at, :] * total).astype(jnp.bfloat16)


EARLY = ((), (0,), (1,), (2,))
LATE = ((0, 1), (1, 2), (0, 2), (0, 1, 2))


def body(tokens, in_weight, short_weight, filter_taps, skip_gain):
    rows = tokens.shape[0]
    side = lax.axis_index("seq")
    place = jnp.stack([lax.axis_index("chan"), side]).astype(jnp.int32)
    precise, forward, inverse = odd_tables()
    held = tokens[None]
    x, y, z = (exchange(held, 0, k) for k in range(3))
    xy, yz, zx = exchange(y, 0, 0), exchange(z, 0, 1), exchange(x, 0, 2)
    early = join([held, x, y, z], xy, yz, first=pltpu.HBM)
    weights = pack(place, in_weight, lax.ppermute(in_weight, "seq", SWAP))
    other_taps = lax.ppermute(filter_taps, "seq", SWAP)
    lag = pl.pallas_call(
        lag_kernel,
        out_shape=jax.ShapeDtypeStruct((2 * BLOCK, 2 * rows // BLOCK * LANES), jnp.float32),
        compiler_params=pltpu.CompilerParams(vmem_limit_bytes=16 << 20),
    )(jnp.where(side == 0, filter_taps, other_taps), jnp.where(side == 0, other_taps, filter_taps), precise)
    late = join([xy, yz, zx, exchange(yz, 0, 0)], weights, lag)

    def at(near, far):
        return tuple((n, far) for n in near)

    acc = project(place, [early, late], [at(EARLY, ()), at(LATE, ())], weights, None, False)
    firsts = [[exchange(h, 1, k) for k in range(3)] for h in (early, late)]
    every = (0, 1, 2)
    second0 = [exchange(after(firsts[0][(k + 1) % 3], acc), 1, k) for k in range(3)]
    acc = project(place, firsts[0], [at(EARLY, (k,)) for k in range(3)], weights, acc, False)
    second1 = [exchange(after(firsts[1][(k + 1) % 3], acc), 1, k) for k in range(3)]
    acc = project(place, firsts[1], [at(LATE, (k,)) for k in range(3)], weights, acc, False)
    pairs = ((0, 1), (1, 2), (0, 2))
    thirds = [exchange(after(second0[1], acc), 1, 0)]
    acc = project(place, second0, [at(EARLY, p) for p in pairs], weights, acc, False)
    thirds += [exchange(after(second1[0], acc)[:3], 1, 2), exchange(after(second1[2], acc)[3:], 1, 1)]
    names = [at(LATE, p) for p in pairs]
    acc = project(place, second1, names, weights, acc, False)
    names = [at(EARLY, every), at(LATE[:3], every), at(LATE[3:], every)]
    projected = [project(place, thirds, names, weights, acc, True)]
    before = [lax.ppermute(p, "seq", [(0, 1)]) for p in projected]
    per = rows // BLOCK
    return pl.pallas_call(
        functools.partial(mix_kernel, parts=len(projected)),
        out_shape=jax.ShapeDtypeStruct((rows, LANES), jnp.bfloat16),
        scratch_shapes=[
            pltpu.VMEM((rows + 8, 3 * LANES), jnp.float32),
            pltpu.VMEM((rows + 8, 3 * LANES), jnp.float32),
            pltpu.VMEM((rows, LANES), jnp.float32),
            pltpu.VMEM((rows, LANES), jnp.float32),
            pltpu.VMEM((2 * BLOCK, 2 * per * LANES), jnp.float32),
            pltpu.VMEM((2 * BLOCK, per * LANES), jnp.float32),
        ],
        compiler_params=pltpu.CompilerParams(vmem_limit_bytes=16 << 20),
    )(*projected, *before, lag, short_weight, skip_gain.reshape(1, LANES), forward, inverse)


def solution(mesh):
    in_specs = (
        P("seq", "chan"),
        P(None, "seq", "chan"),
        P(None, None, "chan"),
        P("seq", "chan"),
        P("chan"),
    )
    out_specs = P("seq", "chan")
    return jax.shard_map(body, mesh=mesh, in_specs=in_specs, out_specs=out_specs, check_vma=False)
```
